32 devices in a mesh: groups: 2 (over x), seq: 16 (over z, y, core).
Axes of the slice: x: 2, y: 2, z: 4, core: 2. Of those that a mesh axis runs over, the one named last changes fastest.
Arguments:
- query_rows: bfloat16 [8192, 1024], P(('groups', 'seq')), parts along dimension 0, may hold values from -25 to 25
- key_rows: bfloat16 [8192, 1024], P(('groups', 'seq')), parts along dimension 0, may hold values from -18 to 18
- value_rows: bfloat16 [8192, 1024], P(('groups', 'seq')), parts along dimension 0, may hold values from -18 to 18
- segment_ids: int32 [8192], P(('groups', 'seq')), parts along dimension 0, may hold values from 0 to 2, never falling along the last dimension, each value on 1 to 2560 neighbouring positions
- out_weight: bfloat16 [1024, 1024], replicated, may hold values from -0.1875 to 0.1875
Outputs:
- attended: bfloat16 [8192, 1024], P(('groups', 'seq')), parts along dimension 0
The draws below stay inside these ranges and needn't reach their ends.
There are 2 independent parts, one for each index of `groups`. The reference program is written for one: setup_inputs(seed, part) draws one part's arguments, and reference() takes and returns one part's arrays. A program takes and returns all parts, laid end to end along the dimension named above; an argument that names none is the same for every part. Nothing has to cross between parts.
Inputs may be any that keep to these rules, and one draw needn't show every extreme that they name: `segment_ids`: ids never fall along the sequence; there are three transcripts, one of exactly 2560 tokens.
All inputs are finite; a program needn't handle non-finite values.
Results may differ from the reference program's by a relative error of at most 0.0051.
Values may be sent and summed in bfloat16 or wider, within the bound.
A program may use at most 128 MiB of HBM per device.

```python
import math
import jax
import jax.numpy as jnp
import numpy as np
from jax import lax

H = 16
DH = 64
TILE = 128
TOK_DEV = 256
TOKENS = 4096
SHARD_BITS = 1
SEQ_BITS = 4
N_SEQ = 16


def smooth_rows(seed_key, amplitude):
    waves = jax.random.randint(jax.random.fold_in(seed_key, 1), (1, H * DH), 1, 5).astype(jnp.float32)
    offsets = jax.random.uniform(jax.random.fold_in(seed_key, 2), (1, H * DH), dtype=jnp.float32, minval=0.0, maxval=2.0 * math.pi)
    positions = jnp.arange(TOKENS).astype(jnp.float32)[:, None]
    return amplitude * jnp.sin(2.0 * math.pi * waves * positions / TOKENS + offsets)


def block_offsets(seed_key):
    width = H * DH
    total = jnp.zeros((TOKENS, width), dtype=jnp.float32)
    scale_count = (TOKENS // (2 * TILE)).bit_length() - 1
    for level in range(1, scale_count + 1):
        span = 2 ** level
        table = jax.random.uniform(jax.random.fold_in(seed_key, level), (TOKENS // span, 1, width), dtype=jnp.float32, minval=-0.6, maxval=0.6)
        total = (total.reshape(TOKENS // span, span, width) + table).reshape(TOKENS, width)
    return total


def rough_rows(seed_key):
    jitter = jnp.clip(jax.random.normal(jax.random.fold_in(seed_key, 1), (TOKENS, H * DH), dtype=jnp.float32), -5.0, 5.0)
    scales = jnp.exp(jax.random.uniform(jax.random.fold_in(seed_key, 2), (TOKENS, 1), dtype=jnp.float32, minval=math.log(0.3), maxval=math.log(3.0)))
    return jitter * scales


def key_field(seed_key):
    folded = jax.random.fold_in(seed_key, 101)
    surface = rough_rows(jax.random.fold_in(folded, 1)) + smooth_rows(jax.random.fold_in(folded, 2), 1.5) + block_offsets(jax.random.fold_in(folded, 3))
    surface = jnp.clip(surface, -18.0, 18.0)
    return surface


def draw_key_rows(key, part):
    return key_field(key).astype(jnp.bfloat16)


def draw_value_rows(key, part):
    folded = jax.random.fold_in(key, 404)
    surface = rough_rows(jax.random.fold_in(folded, 1)) + smooth_rows(jax.random.fold_in(folded, 2), 2.0) + block_offsets(jax.random.fold_in(folded, 3))
    return jnp.clip(surface, -18.0, 18.0).astype(jnp.bfloat16)


def draw_query_rows(key, part):
    folded = jax.random.fold_in(key, 505)
    jitter = jnp.clip(jax.random.normal(folded, (TOKENS, H * DH), dtype=jnp.float32), -5.0, 5.0)
    return jitter.astype(jnp.bfloat16)


def profile(count, total, most, lean):
    portions = [(1 << 20) // math.isqrt(rank ** lean) + 1 for rank in range(2, count + 1)]
    spare, given = total - most - (count - 1), [1] * (count - 1)
    while spare > 0:
        candidates = [i for i in range(count - 1) if given[i] < most]
        mass, left = sum([portions[i] for i in candidates]), spare
        for i in candidates:
            more = min(most - given[i], max(1, left * portions[i] // mass), spare)
            given[i] = given[i] + more
            spare = spare - more
    return np.array([most] + given)


def uneven(key, number_of, total, limit, lean):
    if number_of == 2:
        one = jax.random.randint(key, (), max(1, total - limit), min(limit, total - 1) + 1)
        return jnp.stack([one, total - one])
    tallies = jnp.asarray(profile(number_of, total, limit, lean), jnp.int32)
    twos = (number_of - 1) // 2
    donor, receiver = tallies[1:1 + 2 * twos:2], tallies[2:2 + 2 * twos:2]
    room = jnp.minimum(donor - 1, limit - receiver)
    moved = jax.random.randint(jax.random.fold_in(key, 1), (twos,), 0, 1 << 20) % (room + 1)
    tallies = tallies.at[1:1 + 2 * twos:2].set(donor - moved).at[2:2 + 2 * twos:2].set(receiver + moved)
    return tallies[jax.random.permutation(jax.random.fold_in(key, 2), number_of)]


def bell_draw(stream_key, extent, spread, most, kind=jnp.bfloat16):
    array = spread * jax.random.normal(stream_key, extent, jnp.float32)
    return jnp.clip(array, min=-most, max=most).astype(kind)


def setup_inputs(seed: int = 0, part: int = 0) -> dict:
    key_of = jax.random.split(jax.random.key(seed), 6)
    part_splits = jax.random.split(jax.random.fold_in(key_of[5], part), 6)
    query_rows = draw_query_rows(jax.random.fold_in(jax.random.fold_in(key_of[5], part), 71), part)
    key_rows = draw_key_rows(jax.random.fold_in(jax.random.fold_in(key_of[5], part), 71), part)
    value_rows = draw_value_rows(jax.random.fold_in(jax.random.fold_in(key_of[5], part), 71), part)
    segment_ids = jnp.searchsorted(jnp.cumsum(uneven(part_splits[3], 3, TOKENS, 5 * TOKENS // 8, 2)), jnp.arange(TOKENS), side="right").astype(jnp.int32)
    out_weight = bell_draw(key_of[4], (H * DH, H * DH), (H * DH) ** -0.5, 0.1875)
    return dict(query_rows=query_rows, key_rows=key_rows, value_rows=value_rows, segment_ids=segment_ids, out_weight=out_weight)


def level_terms(query_blocks, key_blocks, value_blocks, allowed):
    scores = jnp.einsum('gmhd,gkhd->ghmk', query_blocks.astype(jnp.float32), key_blocks.astype(jnp.float32)) * (DH ** -0.5)
    key_mask = allowed[:, None, :, :]
    largest = jnp.max(jnp.where(key_mask, scores, -1e30), axis=-1)
    weights = jnp.exp(jnp.where(key_mask, scores - largest[..., None], -1e30))
    totals = jnp.sum(weights, axis=-1)
    rounded = weights.astype(jnp.bfloat16)
    weighted = jnp.einsum('ghmk,gkhd->gmhd', rounded.astype(jnp.float32), value_blocks.astype(jnp.float32))
    groups = query_blocks.shape[0]
    members = query_blocks.shape[1]
    largest = jnp.transpose(largest, (0, 2, 1)).reshape(groups * members, H)
    totals = jnp.transpose(totals, (0, 2, 1)).reshape(groups * members, H)
    return largest, totals, weighted.reshape(groups * members, H, DH)


def merge_terms(running, terms):
    new_max = jnp.maximum(running[0], terms[0])
    keep_old = jnp.exp(running[0] - new_max)
    keep_new = jnp.exp(terms[0] - new_max)
    totals = running[1] * keep_old + terms[1] * keep_new
    weighted = running[2] * keep_old[..., None] + terms[2] * keep_new[..., None]
    return new_max, totals, weighted


def pair_mean(source_rows):
    paired = source_rows.reshape(source_rows.shape[0] // 2, 2, source_rows.shape[1]).astype(jnp.float32)
    return ((paired[:, 0] + paired[:, 1]) * 0.5).astype(jnp.bfloat16)


def reference(query_rows, key_rows, value_rows, segment_ids, out_weight):
    width = H * DH
    levels = SHARD_BITS + SEQ_BITS
    seg_plus = segment_ids + 1
    coarse = []
    prev_keys = key_rows
    prev_values = value_rows
    for level_index in range(1, levels):
        factor = 2 ** level_index
        prev_keys = pair_mean(prev_keys)
        prev_values = pair_mean(prev_values)
        seg_pairs = seg_plus.reshape(TOKENS // factor, factor)
        coarse.append((prev_keys, prev_values, seg_pairs[:, 0], seg_pairs[:, factor - 1]))
    key_pad = jnp.pad(key_rows, ((TILE, TILE), (0, 0)))
    value_pad = jnp.pad(value_rows, ((TILE, TILE), (0, 0)))
    seg_pad = jnp.pad(seg_plus, (TILE, TILE))
    tile_count = TOK_DEV // TILE

    def one_shard(shard_index):
        first_row = shard_index * TOK_DEV
        query_shard = lax.dynamic_slice_in_dim(query_rows, first_row, TOK_DEV, 0).reshape(TOK_DEV, H, DH)
        seg_shard = lax.dynamic_slice_in_dim(seg_plus, first_row, TOK_DEV, 0)
        key_span = lax.dynamic_slice_in_dim(key_pad, first_row, TOK_DEV + 2 * TILE, 0).reshape(tile_count + 2, TILE, H, DH)
        value_span = lax.dynamic_slice_in_dim(value_pad, first_row, TOK_DEV + 2 * TILE, 0).reshape(tile_count + 2, TILE, H, DH)
        seg_span = lax.dynamic_slice_in_dim(seg_pad, first_row, TOK_DEV + 2 * TILE, 0).reshape(tile_count + 2, TILE)
        key_window = jnp.concatenate([key_span[:-2], key_span[1:-1], key_span[2:]], axis=1)
        value_window = jnp.concatenate([value_span[:-2], value_span[1:-1], value_span[2:]], axis=1)
        seg_window = jnp.concatenate([seg_span[:-2], seg_span[1:-1], seg_span[2:]], axis=1)
        seg_tiles = seg_shard.reshape(tile_count, TILE)
        allowed = seg_tiles[:, :, None] == seg_window[:, None, :]
        running = level_terms(query_shard.reshape(tile_count, TILE, H, DH), key_window, value_window, allowed)
        for level_index in range(1, levels):
            block_size = TILE * 2 ** level_index
            coarse_keys, coarse_values, seg_first, seg_last = coarse[level_index - 1]
            if 2 * block_size <= TOK_DEV:
                groups = TOK_DEV // block_size
                start_row = first_row // (2 ** level_index)
                row_count = groups * TILE

                def sibling(array_in):
                    taken = lax.dynamic_slice_in_dim(array_in, start_row, row_count, 0)
                    shaped = taken.reshape((groups // 2, 2, TILE) + array_in.shape[1:])
                    return shaped[:, ::-1].reshape((groups, TILE) + array_in.shape[1:])

                key_blocks = sibling(coarse_keys).reshape(groups, TILE, H, DH)
                value_blocks = sibling(coarse_values).reshape(groups, TILE, H, DH)
                first_blocks = sibling(seg_first)
                last_blocks = sibling(seg_last)
                query_blocks = query_shard.reshape(groups, block_size, H, DH)
                seg_blocks = seg_shard.reshape(groups, block_size)
            else:
                block_index = first_row // block_size
                start_row = jnp.bitwise_xor(block_index, 1) * TILE
                key_blocks = lax.dynamic_slice_in_dim(coarse_keys, start_row, TILE, 0).reshape(1, TILE, H, DH)
                value_blocks = lax.dynamic_slice_in_dim(coarse_values, start_row, TILE, 0).reshape(1, TILE, H, DH)
                first_blocks = lax.dynamic_slice_in_dim(seg_first, start_row, TILE, 0)[None]
                last_blocks = lax.dynamic_slice_in_dim(seg_last, start_row, TILE, 0)[None]
                query_blocks = query_shard[None]
                seg_blocks = seg_shard[None]
            allowed = (seg_blocks[:, :, None] == first_blocks[:, None, :]) & (seg_blocks[:, :, None] == last_blocks[:, None, :])
            running = merge_terms(running, level_terms(query_blocks, key_blocks, value_blocks, allowed))
        context = (running[2] / running[1][..., None]).astype(jnp.bfloat16).reshape(TOK_DEV, width)
        return jnp.dot(context, out_weight, preferred_element_type=jnp.float32).astype(jnp.bfloat16)

    result = lax.map(one_shard, jnp.arange(N_SEQ, dtype=jnp.int32))
    return result.reshape(TOKENS, width)
```

```python
import functools
import jax
import jax.numpy as jnp
from jax import lax
from jax.experimental import pallas as pl
from jax.experimental.pallas import tpu as pltpu
from jax.sharding import PartitionSpec as P

H = 16
DH = 64
TILE = 128
LANES = 128
MIN_ROWS = 16
BIG = 2.0**100


def flip(index, mask):
    bit = 0
    while (1 << bit) <= mask:
        if mask & (1 << bit):
            index = index + (1 - 2 * ((index // (1 << bit)) % 2)) * (1 << bit)
        bit += 1
    return index


def level_plan(level):
    rows = max(TILE >> (level - 1), MIN_ROWS)
    shared = max(0, level - 4)
    low = max(1, shared)
    masks = [(1 << (level - 1)) + (c << low) for c in range(1 << max(0, level - 1 - low))]
    return rows, shared, masks, shared == 0 and level > 1


def halve(source):
    rows = source.shape[0]
    row = lax.broadcasted_iota(jnp.int32, (rows // 2, rows), 0)
    col = lax.broadcasted_iota(jnp.int32, (rows // 2, rows), 1)
    pick = jnp.where(col // 2 == row, 0.5, 0.0).astype(jnp.bfloat16)
    return jnp.dot(pick, source, preferred_element_type=jnp.float32).astype(jnp.bfloat16)


def attend(devices, q_ref, k_ref, v_ref, seg_ref, w_hbm, out_ref, kv, left, right, queries,
           query_seg, largest, total, context, w_vmem, w_sem, halo_send, halo_recv, *rest):
    levels = devices.bit_length() - 1
    pieces = rest[:levels]
    blocks = rest[levels : 2 * levels]
    send, recv, fsend, frecv = rest[2 * levels : 2 * levels + 4]
    joins = rest[2 * levels + 4 : -2] if levels > 4 else ()
    if levels > 4:
        jsend, jrecv = rest[-2:]
    me = lax.axis_index("seq")
    width = q_ref.shape[1]
    pairs = width // LANES
    plans = [level_plan(level) for level in range(1, levels + 1)]

    def to(mask):
        return {"seq": flip(me, mask)}

    before = (me + devices - 1) % devices
    after = (me + 1) % devices
    masks = {1}
    for _, _, some, _ in plans:
        masks.update(some)
    for level in range(5, levels + 1):
        masks.add(1 << (level - 5))
    masks = sorted(masks)
    barrier = pltpu.get_barrier_semaphore()
    for mask in masks:
        pl.semaphore_signal(barrier, inc=1, device_id=to(mask),
                            device_id_type=pl.DeviceIdType.MESH)
    for target in (before, after):
        pl.semaphore_signal(barrier, inc=1, device_id={"seq": target},
                            device_id_type=pl.DeviceIdType.MESH)

    w_copy = pltpu.make_async_copy(w_hbm, w_vmem, w_sem)
    w_copy.start()

    tokens = q_ref.shape[0]
    seg = seg_ref[...]
    first = jnp.sum(jnp.where(seg < 1, 1.0, 0.0), axis=1, keepdims=True)
    second = jnp.sum(jnp.where(seg < 2, 1.0, 0.0), axis=1, keepdims=True)
    row = lax.broadcasted_iota(jnp.int32, (tokens, LANES), 0).astype(jnp.float32)
    lane = lax.broadcasted_iota(jnp.int32, (tokens, LANES), 1).astype(jnp.float32)
    row_seg = jnp.where(row >= first, 1.0, 0.0) + jnp.where(row >= second, 1.0, 0.0)
    kv[:, :width] = k_ref[...]
    kv[:, width : width + LANES] = jnp.where(lane == row_seg, -BIG, 0.0).astype(jnp.bfloat16)
    kv[:, width + LANES :] = v_ref[...]
    other = jnp.where(lane == row_seg, 0.0, jnp.where(lane < 4, 1.0, 0.0)).astype(jnp.bfloat16)
    for tile in range(2):
        part = other[tile * TILE : (tile + 1) * TILE]
        query_seg[2 * tile * TILE : (2 * tile + 1) * TILE, :] = part
        query_seg[(2 * tile + 1) * TILE : (2 * tile + 2) * TILE, :] = part

    pl.semaphore_wait(barrier, len(masks) + 2)

    def halo_copy(way):
        source = kv.at[TILE : 2 * TILE] if way == 0 else kv.at[0:TILE]
        return pltpu.make_async_remote_copy(
            src_ref=source, dst_ref=left if way == 0 else right,
            send_sem=halo_send.at[way], recv_sem=halo_recv.at[way],
            device_id={"seq": after if way == 0 else before},
            device_id_type=pl.DeviceIdType.MESH)

    has_right = me < devices - 1
    has_left = me > 0

    @pl.when(has_right)
    def _():
        halo_copy(0).start()

    @pl.when(has_left)
    def _():
        halo_copy(1).start()

    def edge(ref):
        ref[...] = jnp.zeros(ref.shape, ref.dtype)
        spot = lax.broadcasted_iota(jnp.int32, (TILE, LANES), 1)
        ref[:, width : width + LANES] = jnp.where(spot == 3, -BIG, 0.0).astype(jnp.bfloat16)

    @pl.when(me == 0)
    def _():
        edge(left)

    @pl.when(me == devices - 1)
    def _():
        edge(right)

    slots = []
    count = 0
    for _, _, some, _ in plans:
        slots.append(count)
        count += len(some)

    def level_copy(index, c):
        rows, shared, some, _ = plans[index]
        spot = (me % (1 << index)) // (1 << shared) * rows
        return pltpu.make_async_remote_copy(
            src_ref=pieces[index],
            dst_ref=blocks[index].at[pl.ds(pl.multiple_of(spot, MIN_ROWS), rows)],
            send_sem=send.at[slots[index] + c], recv_sem=recv.at[slots[index] + c],
            device_id=to(some[c]), device_id_type=pl.DeviceIdType.MESH)

    def forward_copy(index, c):
        rows, _, some, _ = plans[index]
        spot = pl.multiple_of((flip(me, some[c]) % (1 << index)) * rows, MIN_ROWS)
        part = blocks[index].at[pl.ds(spot, rows)]
        return pltpu.make_async_remote_copy(
            src_ref=part, dst_ref=part,
            send_sem=fsend.at[slots[index] + c], recv_sem=frecv.at[slots[index] + c],
            device_id=to(1), device_id_type=pl.DeviceIdType.MESH)

    for index in range(levels):
        if index == 0:
            pieces[0][...] = halve(kv[...])
        elif index < 4:
            pieces[index][...] = halve(pieces[index - 1][...])
        else:
            join = joins[index - 4]
            mask = 1 << (index - 4)
            half = pl.ds(pl.multiple_of((me // mask) % 2 * MIN_ROWS, MIN_ROWS), MIN_ROWS)
            join[half, :] = pieces[index - 1][...]
            copy = pltpu.make_async_remote_copy(
                src_ref=pieces[index - 1], dst_ref=join.at[half],
                send_sem=jsend.at[index - 4], recv_sem=jrecv.at[index - 4],
                device_id=to(mask), device_id_type=pl.DeviceIdType.MESH)
            copy.start()
            copy.wait()
            pieces[index][...] = halve(join[...])
        for c in range(len(plans[index][2])):
            level_copy(index, c).start()

    ones = jnp.ones((TILE, LANES), jnp.bfloat16)

    def weigh(scores, top, values, keys):
        weights = jnp.exp(scores - top).astype(jnp.bfloat16)
        right_side = jnp.concatenate([values, jnp.ones((keys, LANES), jnp.bfloat16)], axis=1)
        return jnp.dot(weights, right_side, preferred_element_type=jnp.float32)

    def score(left_side, key_part, seg_part):
        right_side = jnp.concatenate([key_part, seg_part], axis=1)
        return lax.dot_general(left_side, right_side, (((1,), (1,)), ((), ())),
                               preferred_element_type=jnp.float32)

    def columns(pair):
        return (pl.ds(pl.multiple_of(pair * LANES, LANES), LANES),
                pl.ds(pl.multiple_of(width + LANES + pair * LANES, LANES), LANES))

    seg_columns = slice(width, width + LANES)

    @pl.loop(0, pairs)
    def _(pair):
        key_cols, value_cols = columns(pair)
        scaled = q_ref[:, key_cols] * jnp.bfloat16(DH**-0.5)
        spot = lax.broadcasted_iota(jnp.int32, (tokens, LANES), 1)
        zero = jnp.zeros_like(scaled)
        low = jnp.where(spot < DH, scaled, zero)
        high = jnp.where(spot < DH, zero, scaled)
        both = jnp.concatenate([low[:TILE], high[:TILE], low[TILE:], high[TILE:]], axis=0)
        queries[pair] = both
        scores = score(jnp.concatenate([both, query_seg[...]], axis=1), kv[:, key_cols],
                       kv[:, seg_columns])
        top = jnp.max(scores, axis=1, keepdims=True)
        largest[pair] = jnp.broadcast_to(top, (2 * tokens, LANES))
        total[pair] = weigh(scores, top, kv[:, value_cols], tokens)

    def far_phase(indices):
        @pl.loop(0, pairs)
        def _(pair):
            key_cols, value_cols = columns(pair)
            left_side = jnp.concatenate([queries[pair], query_seg[...]], axis=1)
            scores = [score(left_side, blocks[i][:, key_cols], blocks[i][:, seg_columns])
                      for i in indices]
            old = largest[pair][:, :1]
            top = old
            for some in scores:
                top = jnp.maximum(top, jnp.max(some, axis=1, keepdims=True))
            acc = total[pair] * jnp.exp(old - top)
            for i, some in zip(indices, scores):
                acc = acc + weigh(some, top, blocks[i][:, value_cols], TILE)
            total[pair] = acc
            largest[pair] = jnp.broadcast_to(top, (2 * tokens, LANES))

    level_copy(0, 0).wait_recv()
    far_phase([0])

    for index in range(1, levels):
        for c in range(len(plans[index][2])):
            level_copy(index, c).wait_recv()
            if plans[index][3]:
                forward_copy(index, c).start()

    @pl.when(has_left)
    def _():
        halo_copy(0).wait_recv()

    @pl.when(has_right)
    def _():
        halo_copy(1).wait_recv()

    @pl.loop(0, pairs)
    def _(pair):
        key_cols, value_cols = columns(pair)
        for tile, halo in ((0, left), (1, right)):
            rows = slice(2 * tile * TILE, 2 * (tile + 1) * TILE)
            left_side = jnp.concatenate([queries[pair, rows], query_seg[rows, :]], axis=1)
            scores = score(left_side, halo[:, key_cols], halo[:, seg_columns])
            old = largest[pair, rows][:, :1]
            top = jnp.maximum(old, jnp.max(scores, axis=1, keepdims=True))
            total[pair, rows] = total[pair, rows] * jnp.exp(old - top) + weigh(
                scores, top, halo[:, value_cols], TILE)
            largest[pair, rows] = jnp.broadcast_to(top, (2 * TILE, LANES))

    for index in range(1, levels):
        if plans[index][3]:
            for c in range(len(plans[index][2])):
                forward_copy(index, c).wait_recv()
    rest_levels = list(range(1, levels))
    while rest_levels:
        far_phase(rest_levels[:3])
        rest_levels = rest_levels[3:]

    @pl.loop(0, pairs)
    def _(pair):
        key_cols, _ = columns(pair)
        spot = lax.broadcasted_iota(jnp.int32, (TILE, LANES), 1)
        for tile in range(2):
            base = 2 * tile * TILE
            one = total[pair, base : base + TILE]
            two = total[pair, base + TILE : base + 2 * TILE]
            top = jnp.where(spot < DH, one[:, :LANES], two[:, :LANES])
            bottom = jnp.where(spot < DH, one[:, LANES:], two[:, LANES:])
            context[tile * TILE : (tile + 1) * TILE, key_cols] = (top / bottom).astype(jnp.bfloat16)

    w_copy.wait()

    @pl.loop(0, out_ref.shape[1] // 256)
    def _(part):
        cols = pl.ds(pl.multiple_of(part * 256, 256), 256)
        out_ref[:, cols] = jnp.dot(context[...], w_vmem[:, cols],
                                   preferred_element_type=jnp.float32).astype(jnp.bfloat16)

    for index in range(levels):
        for c in range(len(plans[index][2])):
            level_copy(index, c).wait_send()
            if plans[index][3]:
                forward_copy(index, c).wait_send()

    @pl.when(has_right)
    def _():
        halo_copy(0).wait_send()

    @pl.when(has_left)
    def _():
        halo_copy(1).wait_send()


def on_device(devices, query_rows, key_rows, value_rows, segment_ids, out_weight):
    tokens, width = query_rows.shape
    levels = devices.bit_length() - 1
    span = 2 * width + LANES
    plans = [level_plan(level) for level in range(1, levels + 1)]
    copies = sum(len(plan[2]) for plan in plans)
    pairs = width // LANES
    bf16 = jnp.bfloat16
    scratch = [
        pltpu.VMEM((tokens, span), bf16),
        pltpu.VMEM((TILE, span), bf16),
        pltpu.VMEM((TILE, span), bf16),
        pltpu.VMEM((pairs, 2 * tokens, LANES), bf16),
        pltpu.VMEM((2 * tokens, LANES), bf16),
        pltpu.VMEM((pairs, 2 * tokens, LANES), jnp.float32),
        pltpu.VMEM((pairs, 2 * tokens, 2 * LANES), jnp.float32),
        pltpu.VMEM((tokens, width), bf16),
        pltpu.VMEM(out_weight.shape, bf16),
        pltpu.SemaphoreType.DMA,
        pltpu.SemaphoreType.DMA((2,)),
        pltpu.SemaphoreType.DMA((2,)),
    ]
    scratch += [pltpu.VMEM((plan[0], span), bf16) for plan in plans]
    scratch += [pltpu.VMEM((TILE, span), bf16) for _ in plans]
    scratch += [pltpu.SemaphoreType.DMA((copies,)) for _ in range(4)]
    if levels > 4:
        scratch += [pltpu.VMEM((2 * MIN_ROWS, span), bf16) for _ in range(levels - 4)]
        scratch += [pltpu.SemaphoreType.DMA((levels - 4,)) for _ in range(2)]
    vmem = pl.BlockSpec(memory_space=pltpu.VMEM)
    return pl.pallas_call(
        functools.partial(attend, devices),
        out_shape=jax.ShapeDtypeStruct((tokens, width), bf16),
        in_specs=[vmem, vmem, vmem, vmem, pl.BlockSpec(memory_space=pl.ANY)],
        out_specs=vmem,
        scratch_shapes=scratch,
        compiler_params=pltpu.CompilerParams(
            collective_id=0, has_side_effects=True, vmem_limit_bytes=48 * 1024 * 1024),
    )(query_rows, key_rows, value_rows, segment_ids.reshape(1, tokens), out_weight)


def solution(mesh):
    rows = P(("groups", "seq"), None)
    return jax.shard_map(
        functools.partial(on_device, mesh.shape["seq"]), mesh=mesh,
        in_specs=(rows, rows, rows, P(("groups", "seq")), P()),
        out_specs=rows, check_vma=False)
```

```python
import functools
import jax
import jax.numpy as jnp
from jax import lax
from jax.experimental import pallas as pl
from jax.experimental.pallas import tpu as pltpu
from jax.sharding import PartitionSpec as P

H = 16
DH = 64
TILE = 128
LANES = 128
MIN_ROWS = 16
BIG = 2.0**100


def flip(index, mask):
    bit = 0
    while (1 << bit) <= mask:
        if mask & (1 << bit):
            index = index + (1 - 2 * ((index // (1 << bit)) % 2)) * (1 << bit)
        bit += 1
    return index


def level_plan(level):
    rows = max(TILE >> (level - 1), MIN_ROWS)
    shared = max(0, level - 4)
    low = max(1, shared)
    masks = [(1 << (level - 1)) + (c << low) for c in range(1 << max(0, level - 1 - low))]
    return rows, shared, masks, shared == 0 and level > 1


def halve(source):
    rows = source.shape[0]
    row = lax.broadcasted_iota(jnp.int32, (rows // 2, rows), 0)
    col = lax.broadcasted_iota(jnp.int32, (rows // 2, rows), 1)
    pick = jnp.where(col // 2 == row, 0.5, 0.0).astype(jnp.bfloat16)
    return jnp.dot(pick, source, preferred_element_type=jnp.float32).astype(jnp.bfloat16)


def attend(devices, q_ref, k_ref, v_ref, seg_ref, w_hbm, out_ref, kv, left, right, queries,
           query_seg, largest, total, context, w_vmem, w_sem, halo_send, halo_recv, *rest):
    levels = devices.bit_length() - 1
    pieces = rest[:levels]
    blocks = rest[levels : 2 * levels]
    send, recv, fsend, frecv = rest[2 * levels : 2 * levels + 4]
    joins = rest[2 * levels + 4 : -2] if levels > 4 else ()
    if levels > 4:
        jsend, jrecv = rest[-2:]
    me = lax.axis_index("seq")
    width = q_ref.shape[1]
    pairs = width // LANES
    plans = [level_plan(level) for level in range(1, levels + 1)]

    def to(mask):
        return {"seq": flip(me, mask)}

    before = (me + devices - 1) % devices
    after = (me + 1) % devices
    masks = {1}
    for _, _, some, _ in plans:
        masks.update(some)
    for level in range(5, levels + 1):
        masks.add(1 << (level - 5))
    masks = sorted(masks)
    barrier = pltpu.get_barrier_semaphore()
    for mask in masks:
        pl.semaphore_signal(barrier, inc=1, device_id=to(mask),
                            device_id_type=pl.DeviceIdType.MESH)
    for target in (before, after):
        pl.semaphore_signal(barrier, inc=1, device_id={"seq": target},
                            device_id_type=pl.DeviceIdType.MESH)

    w_copy = pltpu.make_async_copy(w_hbm, w_vmem, w_sem)
    w_copy.start()

    tokens = q_ref.shape[0]
    seg = seg_ref[...]
    first = jnp.sum(jnp.where(seg < 1, 1.0, 0.0), axis=1, keepdims=True)
    second = jnp.sum(jnp.where(seg < 2, 1.0, 0.0), axis=1, keepdims=True)
    row = lax.broadcasted_iota(jnp.int32, (tokens, LANES), 0).astype(jnp.float32)
    lane = lax.broadcasted_iota(jnp.int32, (tokens, LANES), 1).astype(jnp.float32)
    row_seg = jnp.where(row >= first, 1.0, 0.0) + jnp.where(row >= second, 1.0, 0.0)
    kv[:, :width] = k_ref[...]
    kv[:, width : width + LANES] = jnp.where(lane == row_seg, -BIG, 0.0).astype(jnp.bfloat16)
    kv[:, width + LANES :] = v_ref[...]
    other = jnp.where(lane == row_seg, 0.0, jnp.where(lane < 4, 1.0, 0.0)).astype(jnp.bfloat16)
    query_seg[:tokens, :] = other
    query_seg[tokens:, :] = other

    pl.semaphore_wait(barrier, len(masks) + 2)

    def halo_copy(way):
        source = kv.at[TILE : 2 * TILE] if way == 0 else kv.at[0:TILE]
        return pltpu.make_async_remote_copy(
            src_ref=source, dst_ref=left if way == 0 else right,
            send_sem=halo_send.at[way], recv_sem=halo_recv.at[way],
            device_id={"seq": after if way == 0 else before},
            device_id_type=pl.DeviceIdType.MESH)

    has_right = me < devices - 1
    has_left = me > 0

    def edge(ref):
        ref[...] = jnp.zeros(ref.shape, ref.dtype)
        spot = lax.broadcasted_iota(jnp.int32, (TILE, LANES), 1)
        ref[:, width : width + LANES] = jnp.where(spot == 3, -BIG, 0.0).astype(jnp.bfloat16)

    @pl.when(me == 0)
    def _():
        edge(left)

    @pl.when(me == devices - 1)
    def _():
        edge(right)

    slots = []
    count = 0
    for _, _, some, _ in plans:
        slots.append(count)
        count += len(some)

    def level_copy(index, c):
        rows, shared, some, _ = plans[index]
        spot = (me % (1 << index)) // (1 << shared) * rows
        return pltpu.make_async_remote_copy(
            src_ref=pieces[index],
            dst_ref=blocks[index].at[pl.ds(pl.multiple_of(spot, MIN_ROWS), rows)],
            send_sem=send.at[slots[index] + c], recv_sem=recv.at[slots[index] + c],
            device_id=to(some[c]), device_id_type=pl.DeviceIdType.MESH)

    def forward_copy(index, c):
        rows, _, some, _ = plans[index]
        spot = pl.multiple_of((flip(me, some[c]) % (1 << index)) * rows, MIN_ROWS)
        part = blocks[index].at[pl.ds(spot, rows)]
        return pltpu.make_async_remote_copy(
            src_ref=part, dst_ref=part,
            send_sem=fsend.at[slots[index] + c], recv_sem=frecv.at[slots[index] + c],
            device_id=to(1), device_id_type=pl.DeviceIdType.MESH)

    for index in range(levels):
        if index == 0:
            pieces[0][...] = halve(kv[...])
        elif index < 4:
            pieces[index][...] = halve(pieces[index - 1][...])
        else:
            join = joins[index - 4]
            mask = 1 << (index - 4)
            half = pl.ds(pl.multiple_of((me // mask) % 2 * MIN_ROWS, MIN_ROWS), MIN_ROWS)
            join[half, :] = pieces[index - 1][...]
            copy = pltpu.make_async_remote_copy(
                src_ref=pieces[index - 1], dst_ref=join.at[half],
                send_sem=jsend.at[index - 4], recv_sem=jrecv.at[index - 4],
                device_id=to(mask), device_id_type=pl.DeviceIdType.MESH)
            copy.start()
            copy.wait()
            pieces[index][...] = halve(join[...])
        for c in range(len(plans[index][2])):
            level_copy(index, c).start()

    @pl.when(has_right)
    def _():
        halo_copy(0).start()

    @pl.when(has_left)
    def _():
        halo_copy(1).start()

    spot = lax.broadcasted_iota(jnp.int32, (TILE, LANES), 1)
    low_lanes = spot < DH
    one = jnp.ones((TILE, LANES), jnp.bfloat16)
    zero = jnp.zeros((TILE, LANES), jnp.bfloat16)
    low_ones = jnp.where(low_lanes, one, zero)
    high_ones = jnp.where(low_lanes, zero, one)
    seg_columns = slice(width, width + LANES)

    def columns(pair):
        return (pl.ds(pl.multiple_of(pair * LANES, LANES), LANES),
                pl.ds(pl.multiple_of(width + LANES + pair * LANES, LANES), LANES))

    def score(left_side, ref, base, pair):
        key_cols, _ = columns(pair)
        rows = slice(base, base + TILE)
        right_side = jnp.concatenate([ref[rows, key_cols], ref[rows, seg_columns]], axis=1)
        return lax.dot_general(left_side, right_side, (((1,), (1,)), ((), ())),
                               preferred_element_type=jnp.float32)

    def highest(scores):
        top = scores[0]
        for some in scores[1:]:
            top = jnp.maximum(top, some)
        return jnp.broadcast_to(jnp.max(top, axis=1, keepdims=True), top.shape)

    def weigh(scores, top, spots, pair):
        _, value_cols = columns(pair)
        half = top.shape[0] // 2
        left_side, right_side = [], []
        for some, (ref, base) in zip(scores, spots):
            weights = jnp.exp(some - top).astype(jnp.bfloat16)
            values = ref[slice(base, base + TILE), value_cols]
            left_side += [weights[:half], weights[half:]]
            right_side += [
                jnp.concatenate([jnp.where(low_lanes, values, zero), low_ones], axis=1),
                jnp.concatenate([jnp.where(low_lanes, zero, values), high_ones], axis=1),
            ]
        return jnp.dot(jnp.concatenate(left_side, axis=1), jnp.concatenate(right_side, axis=0),
                       preferred_element_type=jnp.float32)

    def rescale(old, top):
        shrink = jnp.exp(old - top)
        half = top.shape[0] // 2
        lanes = lax.broadcasted_iota(jnp.int32, (half, LANES), 1) < DH
        both = jnp.where(lanes, shrink[:half], shrink[half:])
        return jnp.concatenate([both, both], axis=1)

    near = [(kv, 0), (kv, TILE)]

    level_copy(0, 0).wait_recv()

    @pl.loop(0, pairs)
    def _(pair):
        key_cols, _ = columns(pair)
        scaled = q_ref[:, key_cols] * jnp.bfloat16(DH**-0.5)
        lanes = lax.broadcasted_iota(jnp.int32, (tokens, LANES), 1) < DH
        none = jnp.zeros_like(scaled)
        both = jnp.concatenate([jnp.where(lanes, scaled, none), jnp.where(lanes, none, scaled)],
                               axis=0)
        queries[pair] = both
        spots = near + [(blocks[0], 0)]
        left_side = jnp.concatenate([both, query_seg[...]], axis=1)
        scores = [score(left_side, ref, base, pair) for ref, base in spots]
        top = highest(scores)
        largest[pair] = top
        total[pair] = weigh(scores, top, spots, pair)

    for index in range(1, levels):
        for c in range(len(plans[index][2])):
            level_copy(index, c).wait_recv()
            if plans[index][3]:
                forward_copy(index, c).start()
    for index in range(1, levels):
        if plans[index][3]:
            for c in range(len(plans[index][2])):
                forward_copy(index, c).wait_recv()

    @pl.loop(0, pairs)
    def _(pair):
        left_side = jnp.concatenate([queries[pair], query_seg[...]], axis=1)
        spots = [(blocks[index], 0) for index in range(1, levels)]
        scores = [score(left_side, ref, base, pair) for ref, base in spots]
        old = largest[pair]
        top = jnp.maximum(old, highest(scores))
        largest[pair] = top
        total[pair] = total[pair] * rescale(old, top) + weigh(scores, top, spots, pair)

    @pl.when(has_left)
    def _():
        halo_copy(0).wait_recv()

    @pl.when(has_right)
    def _():
        halo_copy(1).wait_recv()

    @pl.loop(0, pairs)
    def _(pair):
        key_cols, _ = columns(pair)
        for tile, halo in ((0, left), (1, right)):
            one_head = slice(tile * TILE, (tile + 1) * TILE)
            two_head = slice(tokens + tile * TILE, tokens + (tile + 1) * TILE)
            part = jnp.concatenate([queries[pair, one_head], queries[pair, two_head]], axis=0)
            seg_part = jnp.concatenate([query_seg[one_head, :], query_seg[two_head, :]], axis=0)
            scores = [score(jnp.concatenate([part, seg_part], axis=1), halo, 0, pair)]
            old = jnp.concatenate([largest[pair, one_head], largest[pair, two_head]], axis=0)
            top = jnp.maximum(old, highest(scores))
            acc = total[pair, one_head] * rescale(old, top) + weigh(scores, top, [(halo, 0)], pair)
            context[one_head, key_cols] = (acc[:, :LANES] / acc[:, LANES:]).astype(jnp.bfloat16)

    w_copy.wait()

    @pl.loop(0, out_ref.shape[1] // 256)
    def _(part):
        cols = pl.ds(pl.multiple_of(part * 256, 256), 256)
        out_ref[:, cols] = jnp.dot(context[...], w_vmem[:, cols],
                                   preferred_element_type=jnp.float32).astype(jnp.bfloat16)

    for index in range(levels):
        for c in range(len(plans[index][2])):
            level_copy(index, c).wait_send()
            if plans[index][3]:
                forward_copy(index, c).wait_send()

    @pl.when(has_right)
    def _():
        halo_copy(0).wait_send()

    @pl.when(has_left)
    def _():
        halo_copy(1).wait_send()


def on_device(devices, query_rows, key_rows, value_rows, segment_ids, out_weight):
    tokens, width = query_rows.shape
    levels = devices.bit_length() - 1
    span = 2 * width + LANES
    plans = [level_plan(level) for level in range(1, levels + 1)]
    copies = sum(len(plan[2]) for plan in plans)
    pairs = width // LANES
    bf16 = jnp.bfloat16
    scratch = [
        pltpu.VMEM((tokens, span), bf16),
        pltpu.VMEM((TILE, span), bf16),
        pltpu.VMEM((TILE, span), bf16),
        pltpu.VMEM((pairs, 2 * tokens, LANES), bf16),
        pltpu.VMEM((2 * tokens, LANES), bf16),
        pltpu.VMEM((pairs, 2 * tokens, LANES), jnp.float32),
        pltpu.VMEM((pairs, tokens, 2 * LANES), jnp.float32),
        pltpu.VMEM((tokens, width), bf16),
        pltpu.VMEM(out_weight.shape, bf16),
        pltpu.SemaphoreType.DMA,
        pltpu.SemaphoreType.DMA((2,)),
        pltpu.SemaphoreType.DMA((2,)),
    ]
    scratch += [pltpu.VMEM((plan[0], span), bf16) for plan in plans]
    scratch += [pltpu.VMEM((TILE, span), bf16) for _ in plans]
    scratch += [pltpu.SemaphoreType.DMA((copies,)) for _ in range(4)]
    if levels > 4:
        scratch += [pltpu.VMEM((2 * MIN_ROWS, span), bf16) for _ in range(levels - 4)]
        scratch += [pltpu.SemaphoreType.DMA((levels - 4,)) for _ in range(2)]
    vmem = pl.BlockSpec(memory_space=pltpu.VMEM)
    return pl.pallas_call(
        functools.partial(attend, devices),
        out_shape=jax.ShapeDtypeStruct((tokens, width), bf16),
        in_specs=[vmem, vmem, vmem, vmem, pl.BlockSpec(memory_space=pl.ANY)],
        out_specs=vmem,
        scratch_shapes=scratch,
        compiler_params=pltpu.CompilerParams(
            collective_id=0, has_side_effects=True, vmem_limit_bytes=48 * 1024 * 1024),
    )(query_rows, key_rows, value_rows, segment_ids.reshape(1, tokens), out_weight)


def solution(mesh):
    rows = P(("groups", "seq"), None)
    return jax.shard_map(
        functools.partial(on_device, mesh.shape["seq"]), mesh=mesh,
        in_specs=(rows, rows, rows, P(("groups", "seq")), P()),
        out_specs=rows, check_vma=False)
```

```python
import functools
import jax
import jax.numpy as jnp
from jax import lax
from jax.experimental import pallas as pl
from jax.experimental.pallas import tpu as pltpu
from jax.sharding import PartitionSpec as P

H = 16
DH = 64
TILE = 128
LANES = 128
MIN_ROWS = 16
BIG = 2.0**100


def flip(index, mask):
    bit = 0
    while (1 << bit) <= mask:
        if mask & (1 << bit):
            index = index + (1 - 2 * ((index // (1 << bit)) % 2)) * (1 << bit)
        bit += 1
    return index


def level_plan(level):
    rows = max(TILE >> (level - 1), MIN_ROWS)
    shared = max(0, level - 4)
    low = max(1, shared)
    masks = [(1 << (level - 1)) + (c << low) for c in range(1 << max(0, level - 1 - low))]
    return rows, shared, masks, shared == 0 and level > 1


def halve(source):
    rows = source.shape[0]
    row = lax.broadcasted_iota(jnp.int32, (rows // 2, rows), 0)
    col = lax.broadcasted_iota(jnp.int32, (rows // 2, rows), 1)
    pick = jnp.where(col // 2 == row, 0.5, 0.0).astype(jnp.bfloat16)
    return jnp.dot(pick, source, preferred_element_type=jnp.float32).astype(jnp.bfloat16)


def attend(devices, q_hbm, k_hbm, v_hbm, seg_hbm, w_hbm, out_ref, q_ref, seg_ref, load_sem, kv, left, right, queries,
           query_seg, largest, total, context, w_vmem, w_sem, halo_send, halo_recv, *rest):
    levels = devices.bit_length() - 1
    pieces = rest[:levels]
    blocks = rest[levels : 2 * levels]
    send, recv, fsend, frecv = rest[2 * levels : 2 * levels + 4]
    joins = rest[2 * levels + 4 : -2] if levels > 4 else ()
    if levels > 4:
        jsend, jrecv = rest[-2:]
    me = lax.axis_index("seq")
    width = q_hbm.shape[1]
    pairs = width // LANES
    plans = [level_plan(level) for level in range(1, levels + 1)]

    def to(mask):
        return {"seq": flip(me, mask)}

    before = (me + devices - 1) % devices
    after = (me + 1) % devices
    masks = {1}
    for _, _, some, _ in plans:
        masks.update(some)
    for level in range(5, levels + 1):
        masks.add(1 << (level - 5))
    masks = sorted(masks)
    barrier = pltpu.get_barrier_semaphore()
    for mask in masks:
        pl.semaphore_signal(barrier, inc=1, device_id=to(mask),
                            device_id_type=pl.DeviceIdType.MESH)
    for target in (before, after):
        pl.semaphore_signal(barrier, inc=1, device_id={"seq": target},
                            device_id_type=pl.DeviceIdType.MESH)

    loads = [
        pltpu.make_async_copy(seg_hbm, seg_ref, load_sem.at[0]),
        pltpu.make_async_copy(k_hbm, kv.at[:, 0:width], load_sem.at[1]),
        pltpu.make_async_copy(v_hbm, kv.at[:, width + LANES : 2 * width + LANES], load_sem.at[2]),
        pltpu.make_async_copy(q_hbm, q_ref, load_sem.at[3]),
    ]
    for load in loads:
        load.start()
    w_copy = pltpu.make_async_copy(w_hbm, w_vmem, w_sem)
    w_copy.start()
    loads[0].wait()

    tokens = q_hbm.shape[0]
    seg = seg_ref[...]
    first = jnp.sum(jnp.where(seg < 1, 1.0, 0.0), axis=1, keepdims=True)
    second = jnp.sum(jnp.where(seg < 2, 1.0, 0.0), axis=1, keepdims=True)
    row = lax.broadcasted_iota(jnp.int32, (tokens, LANES), 0).astype(jnp.float32)
    lane = lax.broadcasted_iota(jnp.int32, (tokens, LANES), 1).astype(jnp.float32)
    row_seg = jnp.where(row >= first, 1.0, 0.0) + jnp.where(row >= second, 1.0, 0.0)
    kv[:, width : width + LANES] = jnp.where(lane == row_seg, -BIG, 0.0).astype(jnp.bfloat16)
    other = jnp.where(lane == row_seg, 0.0, jnp.where(lane < 4, 1.0, 0.0)).astype(jnp.bfloat16)
    query_seg[:tokens, :] = other
    query_seg[tokens:, :] = other

    loads[1].wait()
    loads[2].wait()
    pl.semaphore_wait(barrier, len(masks) + 2)

    def halo_copy(way):
        source = kv.at[TILE : 2 * TILE] if way == 0 else kv.at[0:TILE]
        return pltpu.make_async_remote_copy(
            src_ref=source, dst_ref=left if way == 0 else right,
            send_sem=halo_send.at[way], recv_sem=halo_recv.at[way],
            device_id={"seq": after if way == 0 else before},
            device_id_type=pl.DeviceIdType.MESH)

    has_right = me < devices - 1
    has_left = me > 0

    def edge(ref):
        ref[...] = jnp.zeros(ref.shape, ref.dtype)
        spot = lax.broadcasted_iota(jnp.int32, (TILE, LANES), 1)
        ref[:, width : width + LANES] = jnp.where(spot == 3, -BIG, 0.0).astype(jnp.bfloat16)

    @pl.when(me == 0)
    def _():
        edge(left)

    @pl.when(me == devices - 1)
    def _():
        edge(right)

    slots = []
    count = 0
    for _, _, some, _ in plans:
        slots.append(count)
        count += len(some)

    def level_copy(index, c):
        rows, shared, some, _ = plans[index]
        spot = (me % (1 << index)) // (1 << shared) * rows
        return pltpu.make_async_remote_copy(
            src_ref=pieces[index],
            dst_ref=blocks[index].at[pl.ds(pl.multiple_of(spot, MIN_ROWS), rows)],
            send_sem=send.at[slots[index] + c], recv_sem=recv.at[slots[index] + c],
            device_id=to(some[c]), device_id_type=pl.DeviceIdType.MESH)

    def forward_copy(index, c):
        rows, _, some, _ = plans[index]
        spot = pl.multiple_of((flip(me, some[c]) % (1 << index)) * rows, MIN_ROWS)
        part = blocks[index].at[pl.ds(spot, rows)]
        return pltpu.make_async_remote_copy(
            src_ref=part, dst_ref=part,
            send_sem=fsend.at[slots[index] + c], recv_sem=frecv.at[slots[index] + c],
            device_id=to(1), device_id_type=pl.DeviceIdType.MESH)

    for index in range(levels):
        if index == 0:
            pieces[0][...] = halve(kv[...])
        elif index < 4:
            pieces[index][...] = halve(pieces[index - 1][...])
        else:
            join = joins[index - 4]
            mask = 1 << (index - 4)
            half = pl.ds(pl.multiple_of((me // mask) % 2 * MIN_ROWS, MIN_ROWS), MIN_ROWS)
            join[half, :] = pieces[index - 1][...]
            copy = pltpu.make_async_remote_copy(
                src_ref=pieces[index - 1], dst_ref=join.at[half],
                send_sem=jsend.at[index - 4], recv_sem=jrecv.at[index - 4],
                device_id=to(mask), device_id_type=pl.DeviceIdType.MESH)
            copy.start()
            copy.wait()
            pieces[index][...] = halve(join[...])
        for c in range(len(plans[index][2])):
            level_copy(index, c).start()

    spot = lax.broadcasted_iota(jnp.int32, (TILE, LANES), 1)
    low_lanes = spot < DH
    one = jnp.ones((TILE, LANES), jnp.bfloat16)
    zero = jnp.zeros((TILE, LANES), jnp.bfloat16)
    low_ones = jnp.where(low_lanes, one, zero)
    high_ones = jnp.where(low_lanes, zero, one)
    seg_columns = slice(width, width + LANES)

    def columns(pair):
        return (pl.ds(pl.multiple_of(pair * LANES, LANES), LANES),
                pl.ds(pl.multiple_of(width + LANES + pair * LANES, LANES), LANES))

    def score(left_side, ref, base, pair):
        key_cols, _ = columns(pair)
        rows = slice(base, base + TILE)
        right_side = jnp.concatenate([ref[rows, key_cols], ref[rows, seg_columns]], axis=1)
        return lax.dot_general(left_side, right_side, (((1,), (1,)), ((), ())),
                               preferred_element_type=jnp.float32)

    def highest(scores):
        top = scores[0]
        for some in scores[1:]:
            top = jnp.maximum(top, some)
        return jnp.broadcast_to(jnp.max(top, axis=1, keepdims=True), top.shape)

    def weigh(scores, top, spots, pair):
        _, value_cols = columns(pair)
        half = top.shape[0] // 2
        left_side, right_side = [], []
        for some, (ref, base) in zip(scores, spots):
            weights = jnp.exp(some - top).astype(jnp.bfloat16)
            values = ref[slice(base, base + TILE), value_cols]
            left_side += [weights[:half], weights[half:]]
            right_side += [
                jnp.concatenate([jnp.where(low_lanes, values, zero), low_ones], axis=1),
                jnp.concatenate([jnp.where(low_lanes, zero, values), high_ones], axis=1),
            ]
        return jnp.dot(jnp.concatenate(left_side, axis=1), jnp.concatenate(right_side, axis=0),
                       preferred_element_type=jnp.float32)

    def rescale(old, top):
        shrink = jnp.exp(old - top)
        half = top.shape[0] // 2
        lanes = lax.broadcasted_iota(jnp.int32, (half, LANES), 1) < DH
        both = jnp.where(lanes, shrink[:half], shrink[half:])
        return jnp.concatenate([both, both], axis=1)

    near = [(kv, 0), (kv, TILE)]
    loads[3].wait()

    level_copy(0, 0).wait_recv()

    @pl.loop(0, pairs)
    def _(pair):
        key_cols, _ = columns(pair)
        scaled = q_ref[:, key_cols] * jnp.bfloat16(DH**-0.5)
        lanes = lax.broadcasted_iota(jnp.int32, (tokens, LANES), 1) < DH
        none = jnp.zeros_like(scaled)
        both = jnp.concatenate([jnp.where(lanes, scaled, none), jnp.where(lanes, none, scaled)],
                               axis=0)
        queries[pair] = both
        spots = near + [(blocks[0], 0)]
        left_side = jnp.concatenate([both, query_seg[...]], axis=1)
        scores = [score(left_side, ref, base, pair) for ref, base in spots]
        top = highest(scores)
        largest[pair] = top
        total[pair] = weigh(scores, top, spots, pair)

    for index in range(1, levels):
        for c in range(len(plans[index][2])):
            level_copy(index, c).wait_recv()
            if plans[index][3]:
                forward_copy(index, c).start()
    @pl.when(has_right)
    def _():
        halo_copy(0).start()

    @pl.when(has_left)
    def _():
        halo_copy(1).start()

    for index in range(1, levels):
        if plans[index][3]:
            for c in range(len(plans[index][2])):
                forward_copy(index, c).wait_recv()

    @pl.loop(0, pairs)
    def _(pair):
        left_side = jnp.concatenate([queries[pair], query_seg[...]], axis=1)
        spots = [(blocks[index], 0) for index in range(1, levels)]
        scores = [score(left_side, ref, base, pair) for ref, base in spots]
        old = largest[pair]
        top = jnp.maximum(old, highest(scores))
        largest[pair] = top
        total[pair] = total[pair] * rescale(old, top) + weigh(scores, top, spots, pair)

    @pl.when(has_left)
    def _():
        halo_copy(0).wait_recv()

    @pl.when(has_right)
    def _():
        halo_copy(1).wait_recv()

    @pl.loop(0, pairs)
    def _(pair):
        key_cols, _ = columns(pair)
        for tile, halo in ((0, left), (1, right)):
            one_head = slice(tile * TILE, (tile + 1) * TILE)
            two_head = slice(tokens + tile * TILE, tokens + (tile + 1) * TILE)
            part = jnp.concatenate([queries[pair, one_head], queries[pair, two_head]], axis=0)
            seg_part = jnp.concatenate([query_seg[one_head, :], query_seg[two_head, :]], axis=0)
            scores = [score(jnp.concatenate([part, seg_part], axis=1), halo, 0, pair)]
            old = jnp.concatenate([largest[pair, one_head], largest[pair, two_head]], axis=0)
            top = jnp.maximum(old, highest(scores))
            acc = total[pair, one_head] * rescale(old, top) + weigh(scores, top, [(halo, 0)], pair)
            context[one_head, key_cols] = (acc[:, :LANES] / acc[:, LANES:]).astype(jnp.bfloat16)

    w_copy.wait()

    @pl.loop(0, out_ref.shape[1] // 256)
    def _(part):
        cols = pl.ds(pl.multiple_of(part * 256, 256), 256)
        out_ref[:, cols] = jnp.dot(context[...], w_vmem[:, cols],
                                   preferred_element_type=jnp.float32).astype(jnp.bfloat16)

    for index in range(levels):
        for c in range(len(plans[index][2])):
            level_copy(index, c).wait_send()
            if plans[index][3]:
                forward_copy(index, c).wait_send()

    @pl.when(has_right)
    def _():
        halo_copy(0).wait_send()

    @pl.when(has_left)
    def _():
        halo_copy(1).wait_send()


def on_device(devices, query_rows, key_rows, value_rows, segment_ids, out_weight):
    tokens, width = query_rows.shape
    levels = devices.bit_length() - 1
    span = 2 * width + LANES
    plans = [level_plan(level) for level in range(1, levels + 1)]
    copies = sum(len(plan[2]) for plan in plans)
    pairs = width // LANES
    bf16 = jnp.bfloat16
    scratch = [
        pltpu.VMEM((tokens, width), bf16),
        pltpu.VMEM((1, tokens), jnp.int32),
        pltpu.SemaphoreType.DMA((4,)),
        pltpu.VMEM((tokens, span), bf16),
        pltpu.VMEM((TILE, span), bf16),
        pltpu.VMEM((TILE, span), bf16),
        pltpu.VMEM((pairs, 2 * tokens, LANES), bf16),
        pltpu.VMEM((2 * tokens, LANES), bf16),
        pltpu.VMEM((pairs, 2 * tokens, LANES), jnp.float32),
        pltpu.VMEM((pairs, tokens, 2 * LANES), jnp.float32),
        pltpu.VMEM((tokens, width), bf16),
        pltpu.VMEM(out_weight.shape, bf16),
        pltpu.SemaphoreType.DMA,
        pltpu.SemaphoreType.DMA((2,)),
        pltpu.SemaphoreType.DMA((2,)),
    ]
    scratch += [pltpu.VMEM((plan[0], span), bf16) for plan in plans]
    scratch += [pltpu.VMEM((TILE, span), bf16) for _ in plans]
    scratch += [pltpu.SemaphoreType.DMA((copies,)) for _ in range(4)]
    if levels > 4:
        scratch += [pltpu.VMEM((2 * MIN_ROWS, span), bf16) for _ in range(levels - 4)]
        scratch += [pltpu.SemaphoreType.DMA((levels - 4,)) for _ in range(2)]
    vmem = pl.BlockSpec(memory_space=pltpu.VMEM)
    return pl.pallas_call(
        functools.partial(attend, devices),
        out_shape=jax.ShapeDtypeStruct((tokens, width), bf16),
        in_specs=[pl.BlockSpec(memory_space=pltpu.HBM)] * 5,
        out_specs=vmem,
        scratch_shapes=scratch,
        compiler_params=pltpu.CompilerParams(
            collective_id=0, has_side_effects=True),
    )(query_rows, key_rows, value_rows, segment_ids.reshape(1, tokens), out_weight)


def solution(mesh):
    rows = P(("groups", "seq"), None)
    return jax.shard_map(
        functools.partial(on_device, mesh.shape["seq"]), mesh=mesh,
        in_specs=(rows, rows, rows, P(("groups", "seq")), P()),
        out_specs=rows, check_vma=False)
```

```python
import functools
import jax
import jax.numpy as jnp
from jax import lax
from jax.experimental import pallas as pl
from jax.experimental.pallas import tpu as pltpu
from jax.sharding import PartitionSpec as P

H = 16
DH = 64
TILE = 128
LANES = 128
MIN_ROWS = 16
BIG = 2.0**100


def flip(index, mask):
    bit = 0
    while (1 << bit) <= mask:
        if mask & (1 << bit):
            index = index + (1 - 2 * ((index // (1 << bit)) % 2)) * (1 << bit)
        bit += 1
    return index


def level_plan(level):
    rows = max(TILE >> (level - 1), MIN_ROWS)
    shared = max(0, level - 4)
    low = max(1, shared)
    masks = [(1 << (level - 1)) + (c << low) for c in range(1 << max(0, level - 1 - low))]
    return rows, shared, masks, shared == 0 and level > 1


def halve(source):
    rows = source.shape[0]
    row = lax.broadcasted_iota(jnp.int32, (rows // 2, rows), 0)
    col = lax.broadcasted_iota(jnp.int32, (rows // 2, rows), 1)
    pick = jnp.where(col // 2 == row, 0.5, 0.0).astype(jnp.bfloat16)
    return jnp.dot(pick, source, preferred_element_type=jnp.float32).astype(jnp.bfloat16)


def attend(devices, q_hbm, k_hbm, v_hbm, seg_hbm, w_hbm, out_ref, q_ref, seg_ref, load_sem, kv, left, right, queries,
           query_seg, largest, total, context, w_vmem, w_sem, halo_send, halo_recv, *rest):
    levels = devices.bit_length() - 1
    pieces = rest[:levels]
    blocks = rest[levels : 2 * levels]
    send, recv, fsend, frecv = rest[2 * levels : 2 * levels + 4]
    joins = rest[2 * levels + 4 : -2] if levels > 4 else ()
    if levels > 4:
        jsend, jrecv = rest[-2:]
    me = lax.axis_index("seq")
    width = q_hbm.shape[1]
    pairs = width // LANES
    plans = [level_plan(level) for level in range(1, levels + 1)]

    def to(mask):
        return {"seq": flip(me, mask)}

    before = (me + devices - 1) % devices
    after = (me + 1) % devices
    masks = {1}
    for _, _, some, _ in plans:
        masks.update(some)
    for level in range(5, levels + 1):
        masks.add(1 << (level - 5))
    masks = sorted(masks)
    barrier = pltpu.get_barrier_semaphore()
    for mask in masks:
        pl.semaphore_signal(barrier, inc=1, device_id=to(mask),
                            device_id_type=pl.DeviceIdType.MESH)
    for target in (before, after):
        pl.semaphore_signal(barrier, inc=1, device_id={"seq": target},
                            device_id_type=pl.DeviceIdType.MESH)

    loads = [
        pltpu.make_async_copy(seg_hbm, seg_ref, load_sem.at[0]),
        pltpu.make_async_copy(k_hbm, kv.at[:, 0:width], load_sem.at[1]),
        pltpu.make_async_copy(v_hbm, kv.at[:, width + LANES : 2 * width + LANES], load_sem.at[2]),
        pltpu.make_async_copy(q_hbm, q_ref, load_sem.at[3]),
    ]
    for load in loads:
        load.start()
    w_copy = pltpu.make_async_copy(w_hbm, w_vmem, w_sem)
    w_copy.start()
    loads[0].wait()

    tokens = q_hbm.shape[0]
    seg = seg_ref[...]
    first = jnp.sum(jnp.where(seg < 1, 1.0, 0.0), axis=1, keepdims=True)
    second = jnp.sum(jnp.where(seg < 2, 1.0, 0.0), axis=1, keepdims=True)
    row = lax.broadcasted_iota(jnp.int32, (tokens, LANES), 0).astype(jnp.float32)
    lane = lax.broadcasted_iota(jnp.int32, (tokens, LANES), 1).astype(jnp.float32)
    row_seg = jnp.where(row >= first, 1.0, 0.0) + jnp.where(row >= second, 1.0, 0.0)
    kv[:, width : width + LANES] = jnp.where(lane == row_seg, -BIG, 0.0).astype(jnp.bfloat16)
    other = jnp.where(lane == row_seg, 0.0, jnp.where(lane < 4, 1.0, 0.0)).astype(jnp.bfloat16)
    query_seg[:tokens, :] = other
    query_seg[tokens:, :] = other

    loads[1].wait()
    loads[2].wait()
    pl.semaphore_wait(barrier, len(masks) + 2)

    def halo_copy(way):
        source = kv.at[TILE : 2 * TILE] if way == 0 else kv.at[0:TILE]
        return pltpu.make_async_remote_copy(
            src_ref=source, dst_ref=left if way == 0 else right,
            send_sem=halo_send.at[way], recv_sem=halo_recv.at[way],
            device_id={"seq": after if way == 0 else before},
            device_id_type=pl.DeviceIdType.MESH)

    has_right = me < devices - 1
    has_left = me > 0

    def edge(ref):
        ref[...] = jnp.zeros(ref.shape, ref.dtype)
        spot = lax.broadcasted_iota(jnp.int32, (TILE, LANES), 1)
        ref[:, width : width + LANES] = jnp.where(spot == 3, -BIG, 0.0).astype(jnp.bfloat16)

    @pl.when(me == 0)
    def _():
        edge(left)

    @pl.when(me == devices - 1)
    def _():
        edge(right)

    slots = []
    count = 0
    for _, _, some, _ in plans:
        slots.append(count)
        count += len(some)

    def level_copy(index, c):
        rows, shared, some, _ = plans[index]
        spot = (me % (1 << index)) // (1 << shared) * rows
        return pltpu.make_async_remote_copy(
            src_ref=pieces[index],
            dst_ref=blocks[index].at[pl.ds(pl.multiple_of(spot, MIN_ROWS), rows)],
            send_sem=send.at[slots[index] + c], recv_sem=recv.at[slots[index] + c],
            device_id=to(some[c]), device_id_type=pl.DeviceIdType.MESH)

    def forward_copy(index, c):
        rows, _, some, _ = plans[index]
        spot = pl.multiple_of((flip(me, some[c]) % (1 << index)) * rows, MIN_ROWS)
        part = blocks[index].at[pl.ds(spot, rows)]
        return pltpu.make_async_remote_copy(
            src_ref=part, dst_ref=part,
            send_sem=fsend.at[slots[index] + c], recv_sem=frecv.at[slots[index] + c],
            device_id=to(1), device_id_type=pl.DeviceIdType.MESH)

    for index in range(levels):
        if index == 0:
            pieces[0][...] = halve(kv[...])
        elif index < 4:
            pieces[index][...] = halve(pieces[index - 1][...])
        else:
            join = joins[index - 4]
            mask = 1 << (index - 4)
            half = pl.ds(pl.multiple_of((me // mask) % 2 * MIN_ROWS, MIN_ROWS), MIN_ROWS)
            join[half, :] = pieces[index - 1][...]
            copy = pltpu.make_async_remote_copy(
                src_ref=pieces[index - 1], dst_ref=join.at[half],
                send_sem=jsend.at[index - 4], recv_sem=jrecv.at[index - 4],
                device_id=to(mask), device_id_type=pl.DeviceIdType.MESH)
            copy.start()
            copy.wait()
            pieces[index][...] = halve(join[...])
        for c in range(len(plans[index][2])):
            level_copy(index, c).start()

    spot = lax.broadcasted_iota(jnp.int32, (TILE, LANES), 1)
    low_lanes = spot < DH
    one = jnp.ones((TILE, LANES), jnp.bfloat16)
    zero = jnp.zeros((TILE, LANES), jnp.bfloat16)
    low_ones = jnp.where(low_lanes, one, zero)
    high_ones = jnp.where(low_lanes, zero, one)
    seg_columns = slice(width, width + LANES)

    def columns(pair):
        return (pl.ds(pl.multiple_of(pair * LANES, LANES), LANES),
                pl.ds(pl.multiple_of(width + LANES + pair * LANES, LANES), LANES))

    def score(left_side, ref, base, pair):
        key_cols, _ = columns(pair)
        rows = slice(base, base + TILE)
        right_side = jnp.concatenate([ref[rows, key_cols], ref[rows, seg_columns]], axis=1)
        return lax.dot_general(left_side, right_side, (((1,), (1,)), ((), ())),
                               preferred_element_type=jnp.float32)

    def highest(scores):
        top = scores[0]
        for some in scores[1:]:
            top = jnp.maximum(top, some)
        return jnp.broadcast_to(jnp.max(top, axis=1, keepdims=True), top.shape)

    def weigh(scores, top, spots, pair):
        _, value_cols = columns(pair)
        half = top.shape[0] // 2
        left_side, right_side = [], []
        for some, (ref, base) in zip(scores, spots):
            weights = jnp.exp(some - top).astype(jnp.bfloat16)
            values = ref[slice(base, base + TILE), value_cols]
            left_side += [weights[:half], weights[half:]]
            right_side += [
                jnp.concatenate([jnp.where(low_lanes, values, zero), low_ones], axis=1),
                jnp.concatenate([jnp.where(low_lanes, zero, values), high_ones], axis=1),
            ]
        return jnp.dot(jnp.concatenate(left_side, axis=1), jnp.concatenate(right_side, axis=0),
                       preferred_element_type=jnp.float32)

    def rescale(old, top):
        shrink = jnp.exp(old - top)
        half = top.shape[0] // 2
        lanes = lax.broadcasted_iota(jnp.int32, (half, LANES), 1) < DH
        both = jnp.where(lanes, shrink[:half], shrink[half:])
        return jnp.concatenate([both, both], axis=1)

    near = [(kv, 0), (kv, TILE)]
    loads[3].wait()

    level_copy(0, 0).wait_recv()

    @pl.loop(0, pairs, unroll=2)
    def _(pair):
        key_cols, _ = columns(pair)
        scaled = q_ref[:, key_cols] * jnp.bfloat16(DH**-0.5)
        lanes = lax.broadcasted_iota(jnp.int32, (tokens, LANES), 1) < DH
        none = jnp.zeros_like(scaled)
        both = jnp.concatenate([jnp.where(lanes, scaled, none), jnp.where(lanes, none, scaled)],
                               axis=0)
        queries[pair] = both
        spots = near + [(blocks[0], 0)]
        left_side = jnp.concatenate([both, query_seg[...]], axis=1)
        scores = [score(left_side, ref, base, pair) for ref, base in spots]
        top = highest(scores)
        largest[pair] = top
        total[pair] = weigh(scores, top, spots, pair)

    @pl.when(has_right)
    def _():
        halo_copy(0).start()
    for index in range(1, levels):
        for c in range(len(plans[index][2])):
            level_copy(index, c).wait_recv()
            if plans[index][3]:
                forward_copy(index, c).start()

    @pl.when(has_left)
    def _():
        halo_copy(1).start()

    for index in range(1, levels):
        if plans[index][3]:
            for c in range(len(plans[index][2])):
                forward_copy(index, c).wait_recv()

    @pl.loop(0, pairs, unroll=2)
    def _(pair):
        left_side = jnp.concatenate([queries[pair], query_seg[...]], axis=1)
        spots = [(blocks[index], 0) for index in range(1, levels)]
        scores = [score(left_side, ref, base, pair) for ref, base in spots]
        old = largest[pair]
        top = jnp.maximum(old, highest(scores))
        largest[pair] = top
        total[pair] = total[pair] * rescale(old, top) + weigh(scores, top, spots, pair)

    @pl.when(has_left)
    def _():
        halo_copy(0).wait_recv()

    @pl.when(has_right)
    def _():
        halo_copy(1).wait_recv()

    @pl.loop(0, pairs, unroll=8)
    def _(pair):
        key_cols, _ = columns(pair)
        for tile, halo in ((0, left), (1, right)):
            one_head = slice(tile * TILE, (tile + 1) * TILE)
            two_head = slice(tokens + tile * TILE, tokens + (tile + 1) * TILE)
            part = jnp.concatenate([queries[pair, one_head], queries[pair, two_head]], axis=0)
            seg_part = jnp.concatenate([query_seg[one_head, :], query_seg[two_head, :]], axis=0)
            scores = [score(jnp.concatenate([part, seg_part], axis=1), halo, 0, pair)]
            old = jnp.concatenate([largest[pair, one_head], largest[pair, two_head]], axis=0)
            top = jnp.maximum(old, highest(scores))
            acc = total[pair, one_head] * rescale(old, top) + weigh(scores, top, [(halo, 0)], pair)
            context[one_head, key_cols] = (acc[:, :LANES] / acc[:, LANES:]).astype(jnp.bfloat16)

    w_copy.wait()

    @pl.loop(0, out_ref.shape[1] // 256)
    def _(part):
        cols = pl.ds(pl.multiple_of(part * 256, 256), 256)
        out_ref[:, cols] = jnp.dot(context[...], w_vmem[:, cols],
                                   preferred_element_type=jnp.float32).astype(jnp.bfloat16)

    for index in range(levels):
        for c in range(len(plans[index][2])):
            level_copy(index, c).wait_send()
            if plans[index][3]:
                forward_copy(index, c).wait_send()

    @pl.when(has_right)
    def _():
        halo_copy(0).wait_send()

    @pl.when(has_left)
    def _():
        halo_copy(1).wait_send()


def on_device(devices, query_rows, key_rows, value_rows, segment_ids, out_weight):
    tokens, width = query_rows.shape
    levels = devices.bit_length() - 1
    span = 2 * width + LANES
    plans = [level_plan(level) for level in range(1, levels + 1)]
    copies = sum(len(plan[2]) for plan in plans)
    pairs = width // LANES
    bf16 = jnp.bfloat16
    scratch = [
        pltpu.VMEM((tokens, width), bf16),
        pltpu.VMEM((1, tokens), jnp.int32),
        pltpu.SemaphoreType.DMA((4,)),
        pltpu.VMEM((tokens, span), bf16),
        pltpu.VMEM((TILE, span), bf16),
        pltpu.VMEM((TILE, span), bf16),
        pltpu.VMEM((pairs, 2 * tokens, LANES), bf16),
        pltpu.VMEM((2 * tokens, LANES), bf16),
        pltpu.VMEM((pairs, 2 * tokens, LANES), jnp.float32),
        pltpu.VMEM((pairs, tokens, 2 * LANES), jnp.float32),
        pltpu.VMEM((tokens, width), bf16),
        pltpu.VMEM(out_weight.shape, bf16),
        pltpu.SemaphoreType.DMA,
        pltpu.SemaphoreType.DMA((2,)),
        pltpu.SemaphoreType.DMA((2,)),
    ]
    scratch += [pltpu.VMEM((plan[0], span), bf16) for plan in plans]
    scratch += [pltpu.VMEM((TILE, span), bf16) for _ in plans]
    scratch += [pltpu.SemaphoreType.DMA((copies,)) for _ in range(4)]
    if levels > 4:
        scratch += [pltpu.VMEM((2 * MIN_ROWS, span), bf16) for _ in range(levels - 4)]
        scratch += [pltpu.SemaphoreType.DMA((levels - 4,)) for _ in range(2)]
    vmem = pl.BlockSpec(memory_space=pltpu.VMEM)
    return pl.pallas_call(
        functools.partial(attend, devices),
        out_shape=jax.ShapeDtypeStruct((tokens, width), bf16),
        in_specs=[pl.BlockSpec(memory_space=pltpu.HBM)] * 5,
        out_specs=vmem,
        scratch_shapes=scratch,
        compiler_params=pltpu.CompilerParams(
            collective_id=0, has_side_effects=True),
    )(query_rows, key_rows, value_rows, segment_ids.reshape(1, tokens), out_weight)


def solution(mesh):
    rows = P(("groups", "seq"), None)
    return jax.shard_map(
        functools.partial(on_device, mesh.shape["seq"]), mesh=mesh,
        in_specs=(rows, rows, rows, P(("groups", "seq")), P()),
        out_specs=rows, check_vma=False)
```

```python
import functools
import jax
import jax.numpy as jnp
from jax import lax
from jax.experimental import pallas as pl
from jax.experimental.pallas import tpu as pltpu
from jax.sharding import PartitionSpec as P

H = 16
DH = 64
TILE = 128
LANES = 128
MIN_ROWS = 16
BIG = 2.0**100


def flip(index, mask):
    bit = 0
    while (1 << bit) <= mask:
        if mask & (1 << bit):
            index = index + (1 - 2 * ((index // (1 << bit)) % 2)) * (1 << bit)
        bit += 1
    return index


def level_plan(level):
    rows = max(TILE >> (level - 1), MIN_ROWS)
    shared = max(0, level - 4)
    low = max(1, shared)
    masks = [(1 << (level - 1)) + (c << low) for c in range(1 << max(0, level - 1 - low))]
    return rows, shared, masks, shared == 0 and level > 1


def halve(source):
    rows = source.shape[0]
    row = lax.broadcasted_iota(jnp.int32, (rows // 2, rows), 0)
    col = lax.broadcasted_iota(jnp.int32, (rows // 2, rows), 1)
    pick = jnp.where(col // 2 == row, 0.5, 0.0).astype(jnp.bfloat16)
    return jnp.dot(pick, source, preferred_element_type=jnp.float32).astype(jnp.bfloat16)


def attend(devices, q_hbm, k_hbm, v_hbm, seg_hbm, w_hbm, out_ref, q_ref, seg_ref, load_sem, kv, left, right, queries,
           query_seg, largest, total, context, w_vmem, w_sem, halo_send, halo_recv, *rest):
    levels = devices.bit_length() - 1
    pieces = rest[:levels]
    blocks = rest[levels : 2 * levels]
    send, recv, fsend, frecv = rest[2 * levels : 2 * levels + 4]
    joins = rest[2 * levels + 4 : -2] if levels > 4 else ()
    if levels > 4:
        jsend, jrecv = rest[-2:]
    me = lax.axis_index("seq")
    width = q_hbm.shape[1]
    pairs = width // LANES
    plans = [level_plan(level) for level in range(1, levels + 1)]

    def to(mask):
        return {"seq": flip(me, mask)}

    before = (me + devices - 1) % devices
    after = (me + 1) % devices
    masks = {1}
    for _, _, some, _ in plans:
        masks.update(some)
    for level in range(5, levels + 1):
        masks.add(1 << (level - 5))
    masks = sorted(masks)
    barrier = pltpu.get_barrier_semaphore()
    for mask in masks:
        pl.semaphore_signal(barrier, inc=1, device_id=to(mask),
                            device_id_type=pl.DeviceIdType.MESH)
    for target in (before, after):
        pl.semaphore_signal(barrier, inc=1, device_id={"seq": target},
                            device_id_type=pl.DeviceIdType.MESH)

    loads = [
        pltpu.make_async_copy(seg_hbm, seg_ref, load_sem.at[0]),
        pltpu.make_async_copy(k_hbm, kv.at[:, 0:width], load_sem.at[1]),
        pltpu.make_async_copy(v_hbm, kv.at[:, width + LANES : 2 * width + LANES], load_sem.at[2]),
        pltpu.make_async_copy(q_hbm, q_ref, load_sem.at[3]),
    ]
    for load in loads:
        load.start()
    w_copy = pltpu.make_async_copy(w_hbm, w_vmem, w_sem)
    w_copy.start()
    loads[0].wait()

    tokens = q_hbm.shape[0]
    seg = seg_ref[...]
    first = jnp.sum(jnp.where(seg < 1, 1.0, 0.0), axis=1, keepdims=True)
    second = jnp.sum(jnp.where(seg < 2, 1.0, 0.0), axis=1, keepdims=True)
    row = lax.broadcasted_iota(jnp.int32, (tokens, LANES), 0).astype(jnp.float32)
    lane = lax.broadcasted_iota(jnp.int32, (tokens, LANES), 1).astype(jnp.float32)
    row_seg = jnp.where(row >= first, 1.0, 0.0) + jnp.where(row >= second, 1.0, 0.0)
    kv[:, width : width + LANES] = jnp.where(lane == row_seg, -BIG, 0.0).astype(jnp.bfloat16)
    other = jnp.where(lane == row_seg, 0.0, jnp.where(lane < 4, 1.0, 0.0)).astype(jnp.bfloat16)
    query_seg[:tokens, :] = other
    query_seg[tokens:, :] = other

    loads[1].wait()
    loads[2].wait()
    pl.semaphore_wait(barrier, len(masks) + 2)

    def halo_copy(way):
        source = kv.at[TILE : 2 * TILE] if way == 0 else kv.at[0:TILE]
        return pltpu.make_async_remote_copy(
            src_ref=source, dst_ref=left if way == 0 else right,
            send_sem=halo_send.at[way], recv_sem=halo_recv.at[way],
            device_id={"seq": after if way == 0 else before},
            device_id_type=pl.DeviceIdType.MESH)

    has_right = me < devices - 1
    has_left = me > 0

    def edge(ref):
        ref[...] = jnp.zeros(ref.shape, ref.dtype)
        spot = lax.broadcasted_iota(jnp.int32, (TILE, LANES), 1)
        ref[:, width : width + LANES] = jnp.where(spot == 3, -BIG, 0.0).astype(jnp.bfloat16)

    @pl.when(me == 0)
    def _():
        edge(left)

    @pl.when(me == devices - 1)
    def _():
        edge(right)

    slots = []
    count = 0
    for _, _, some, _ in plans:
        slots.append(count)
        count += len(some)

    def level_copy(index, c):
        rows, shared, some, _ = plans[index]
        spot = (me % (1 << index)) // (1 << shared) * rows
        return pltpu.make_async_remote_copy(
            src_ref=pieces[index],
            dst_ref=blocks[index].at[pl.ds(pl.multiple_of(spot, MIN_ROWS), rows)],
            send_sem=send.at[slots[index] + c], recv_sem=recv.at[slots[index] + c],
            device_id=to(some[c]), device_id_type=pl.DeviceIdType.MESH)

    def forward_copy(index, c):
        rows, _, some, _ = plans[index]
        spot = pl.multiple_of((flip(me, some[c]) % (1 << index)) * rows, MIN_ROWS)
        part = blocks[index].at[pl.ds(spot, rows)]
        return pltpu.make_async_remote_copy(
            src_ref=part, dst_ref=part,
            send_sem=fsend.at[slots[index] + c], recv_sem=frecv.at[slots[index] + c],
            device_id=to(1), device_id_type=pl.DeviceIdType.MESH)

    for index in range(levels):
        if index == 0:
            pieces[0][...] = halve(kv[...])
        elif index < 4:
            pieces[index][...] = halve(pieces[index - 1][...])
        else:
            join = joins[index - 4]
            mask = 1 << (index - 4)
            half = pl.ds(pl.multiple_of((me // mask) % 2 * MIN_ROWS, MIN_ROWS), MIN_ROWS)
            join[half, :] = pieces[index - 1][...]
            copy = pltpu.make_async_remote_copy(
                src_ref=pieces[index - 1], dst_ref=join.at[half],
                send_sem=jsend.at[index - 4], recv_sem=jrecv.at[index - 4],
                device_id=to(mask), device_id_type=pl.DeviceIdType.MESH)
            copy.start()
            copy.wait()
            pieces[index][...] = halve(join[...])
        for c in range(len(plans[index][2])):
            level_copy(index, c).start()

    spot = lax.broadcasted_iota(jnp.int32, (TILE, LANES), 1)
    low_lanes = spot < DH
    one = jnp.ones((TILE, LANES), jnp.bfloat16)
    zero = jnp.zeros((TILE, LANES), jnp.bfloat16)
    low_ones = jnp.where(low_lanes, one, zero)
    high_ones = jnp.where(low_lanes, zero, one)
    seg_columns = slice(width, width + LANES)

    def columns(pair):
        return (pl.ds(pl.multiple_of(pair * LANES, LANES), LANES),
                pl.ds(pl.multiple_of(width + LANES + pair * LANES, LANES), LANES))

    def score(left_side, ref, base, pair):
        key_cols, _ = columns(pair)
        rows = slice(base, base + TILE)
        right_side = jnp.concatenate([ref[rows, key_cols], ref[rows, seg_columns]], axis=1)
        return lax.dot_general(left_side, right_side, (((1,), (1,)), ((), ())),
                               preferred_element_type=jnp.float32)

    def highest(scores):
        top = scores[0]
        for some in scores[1:]:
            top = jnp.maximum(top, some)
        return jnp.broadcast_to(jnp.max(top, axis=1, keepdims=True), top.shape)

    def weigh(scores, top, spots, pair):
        _, value_cols = columns(pair)
        half = top.shape[0] // 2
        left_side, right_side = [], []
        for some, (ref, base) in zip(scores, spots):
            weights = jnp.exp(some - top).astype(jnp.bfloat16)
            values = ref[slice(base, base + TILE), value_cols]
            left_side += [weights[:half], weights[half:]]
            right_side += [
                jnp.concatenate([jnp.where(low_lanes, values, zero), low_ones], axis=1),
                jnp.concatenate([jnp.where(low_lanes, zero, values), high_ones], axis=1),
            ]
        return jnp.dot(jnp.concatenate(left_side, axis=1), jnp.concatenate(right_side, axis=0),
                       preferred_element_type=jnp.float32)

    def rescale(old, top):
        shrink = jnp.exp(old - top)
        half = top.shape[0] // 2
        lanes = lax.broadcasted_iota(jnp.int32, (half, LANES), 1) < DH
        both = jnp.where(lanes, shrink[:half], shrink[half:])
        return jnp.concatenate([both, both], axis=1)

    near = [(kv, 0), (kv, TILE)]
    loads[3].wait()

    level_copy(0, 0).wait_recv()

    @pl.loop(0, pairs, unroll=4)
    def _(pair):
        key_cols, _ = columns(pair)
        scaled = q_ref[:, key_cols] * jnp.bfloat16(DH**-0.5)
        lanes = lax.broadcasted_iota(jnp.int32, (tokens, LANES), 1) < DH
        none = jnp.zeros_like(scaled)
        both = jnp.concatenate([jnp.where(lanes, scaled, none), jnp.where(lanes, none, scaled)],
                               axis=0)
        queries[pair] = both
        spots = near + [(blocks[0], 0)]
        left_side = jnp.concatenate([both, query_seg[...]], axis=1)
        scores = [score(left_side, ref, base, pair) for ref, base in spots]
        top = highest(scores)
        largest[pair] = top
        total[pair] = weigh(scores, top, spots, pair)

    @pl.when(has_right)
    def _():
        halo_copy(0).start()
    for index in range(1, levels):
        for c in range(len(plans[index][2])):
            level_copy(index, c).wait_recv()
            if plans[index][3]:
                forward_copy(index, c).start()

    @pl.when(has_left)
    def _():
        halo_copy(1).start()

    for index in range(1, levels):
        if plans[index][3]:
            for c in range(len(plans[index][2])):
                forward_copy(index, c).wait_recv()

    @pl.loop(0, pairs, unroll=4)
    def _(pair):
        left_side = jnp.concatenate([queries[pair], query_seg[...]], axis=1)
        spots = [(blocks[index], 0) for index in range(1, levels)]
        scores = [score(left_side, ref, base, pair) for ref, base in spots]
        old = largest[pair]
        top = jnp.maximum(old, highest(scores))
        largest[pair] = top
        total[pair] = total[pair] * rescale(old, top) + weigh(scores, top, spots, pair)

    def near_phase(pair, tile, halo):
        key_cols, _ = columns(pair)
        one_head = slice(tile * TILE, (tile + 1) * TILE)
        two_head = slice(tokens + tile * TILE, tokens + (tile + 1) * TILE)
        part = jnp.concatenate([queries[pair, one_head], queries[pair, two_head]], axis=0)
        seg_part = jnp.concatenate([query_seg[one_head, :], query_seg[two_head, :]], axis=0)
        scores = [score(jnp.concatenate([part, seg_part], axis=1), halo, 0, pair)]
        old = jnp.concatenate([largest[pair, one_head], largest[pair, two_head]], axis=0)
        top = jnp.maximum(old, highest(scores))
        acc = total[pair, one_head] * rescale(old, top) + weigh(scores, top, [(halo, 0)], pair)
        context[one_head, key_cols] = (acc[:, :LANES] / acc[:, LANES:]).astype(jnp.bfloat16)

    @pl.when(has_left)
    def _():
        halo_copy(0).wait_recv()

    @pl.loop(0, pairs, unroll=8)
    def _(pair):
        near_phase(pair, 0, left)

    @pl.when(has_right)
    def _():
        halo_copy(1).wait_recv()

    @pl.loop(0, pairs, unroll=8)
    def _(pair):
        near_phase(pair, 1, right)

    w_copy.wait()

    @pl.loop(0, out_ref.shape[1] // 256, unroll=4)
    def _(part):
        cols = pl.ds(pl.multiple_of(part * 256, 256), 256)
        out_ref[:, cols] = jnp.dot(context[...], w_vmem[:, cols],
                                   preferred_element_type=jnp.float32).astype(jnp.bfloat16)

    for index in range(levels):
        for c in range(len(plans[index][2])):
            level_copy(index, c).wait_send()
            if plans[index][3]:
                forward_copy(index, c).wait_send()

    @pl.when(has_right)
    def _():
        halo_copy(0).wait_send()

    @pl.when(has_left)
    def _():
        halo_copy(1).wait_send()


def on_device(devices, query_rows, key_rows, value_rows, segment_ids, out_weight):
    tokens, width = query_rows.shape
    levels = devices.bit_length() - 1
    span = 2 * width + LANES
    plans = [level_plan(level) for level in range(1, levels + 1)]
    copies = sum(len(plan[2]) for plan in plans)
    pairs = width // LANES
    bf16 = jnp.bfloat16
    scratch = [
        pltpu.VMEM((tokens, width), bf16),
        pltpu.VMEM((1, tokens), jnp.int32),
        pltpu.SemaphoreType.DMA((4,)),
        pltpu.VMEM((tokens, span), bf16),
        pltpu.VMEM((TILE, span), bf16),
        pltpu.VMEM((TILE, span), bf16),
        pltpu.VMEM((pairs, 2 * tokens, LANES), bf16),
        pltpu.VMEM((2 * tokens, LANES), bf16),
        pltpu.VMEM((pairs, 2 * tokens, LANES), jnp.float32),
        pltpu.VMEM((pairs, tokens, 2 * LANES), jnp.float32),
        pltpu.VMEM((tokens, width), bf16),
        pltpu.VMEM(out_weight.shape, bf16),
        pltpu.SemaphoreType.DMA,
        pltpu.SemaphoreType.DMA((2,)),
        pltpu.SemaphoreType.DMA((2,)),
    ]
    scratch += [pltpu.VMEM((plan[0], span), bf16) for plan in plans]
    scratch += [pltpu.VMEM((TILE, span), bf16) for _ in plans]
    scratch += [pltpu.SemaphoreType.DMA((copies,)) for _ in range(4)]
    if levels > 4:
        scratch += [pltpu.VMEM((2 * MIN_ROWS, span), bf16) for _ in range(levels - 4)]
        scratch += [pltpu.SemaphoreType.DMA((levels - 4,)) for _ in range(2)]
    vmem = pl.BlockSpec(memory_space=pltpu.VMEM)
    return pl.pallas_call(
        functools.partial(attend, devices),
        out_shape=jax.ShapeDtypeStruct((tokens, width), bf16),
        in_specs=[pl.BlockSpec(memory_space=pltpu.HBM)] * 5,
        out_specs=vmem,
        scratch_shapes=scratch,
        compiler_params=pltpu.CompilerParams(
            collective_id=0, has_side_effects=True),
    )(query_rows, key_rows, value_rows, segment_ids.reshape(1, tokens), out_weight)


def solution(mesh):
    rows = P(("groups", "seq"), None)
    return jax.shard_map(
        functools.partial(on_device, mesh.shape["seq"]), mesh=mesh,
        in_specs=(rows, rows, rows, P(("groups", "seq")), P()),
        out_specs=rows, check_vma=False)
```
